32 devices in a mesh: dp: 8 (over z, y), mp: 4 (over x, core).
Axes of the slice: x: 2, y: 2, z: 4, core: 2. Of those that a mesh axis runs over, the one named last changes fastest.
Arguments:
- hidden_in: bfloat16 [4096, 2048], P(('dp', 'mp')), may hold values from -6 to 6
- lengths: int32 [8, 3], P('dp'), may hold values from 0 to 512, as said below
- norm_gain: float32 [2048], P(('dp', 'mp')), may hold values from 0.25 to 1.75
- norm_shift: float32 [2048], P(('dp', 'mp')), may hold values from -3 to 3
- qkv_weight: bfloat16 [2048, 3, 2048], P('dp', None, 'mp')
- qkv_bias: bfloat16 [3, 32, 64], P(None, 'mp', 'dp'), may hold values from -3 to 3
- proj_weight: bfloat16 [2048, 2048], P('mp', 'dp'), may hold values from -1.5 to 1.5
- proj_bias: float32 [2048], P(('dp', 'mp')), may hold values from -3 to 3
- up_weight: bfloat16 [2048, 8192], P('dp', 'mp'), may hold values from -0.125 to 0.125
- up_bias: bfloat16 [128, 64], P('mp', 'dp'), may hold values from -3 to 3
- down_weight: bfloat16 [8192, 2048], P('mp', 'dp'), may hold values from -0.0625 to 0.0625
- down_bias: float32 [2048], P(('dp', 'mp')), may hold values from -3 to 3
- cotangent: bfloat16 [4096, 2048], P(('dp', 'mp')), may hold values from -6 to 6
Outputs:
- layer_out: bfloat16 [4096, 2048], P(('dp', 'mp'))
- input_grad: float32 [4096, 2048], P(('dp', 'mp'))
- gain_grad: float32 [2048], P(('dp', 'mp'))
- shift_grad: float32 [2048], P(('dp', 'mp'))
- qkv_grad: float32 [2048, 3, 2048], P('dp', None, 'mp')
- qkvbias_grad: float32 [3, 32, 64], P(None, 'mp', 'dp')
- proj_grad: float32 [2048, 2048], P('mp', 'dp')
- projbias_grad: float32 [2048], P(('dp', 'mp'))
- up_grad: float32 [2048, 8192], P('dp', 'mp')
- upbias_grad: float32 [128, 64], P('mp', 'dp')
- down_grad: float32 [8192, 2048], P('mp', 'dp')
- downbias_grad: float32 [2048], P(('dp', 'mp'))
The draws below stay inside these ranges and needn't reach their ends.
Inputs may be any that keep to these rules, and one draw needn't show every extreme that they name: Each row lists the lengths of one group's sequences, nonzero ones first, summing to 512; a group holds 1 to 3 sequences, and in every draw some group holds a single sequence of 512 tokens.
All inputs are finite; a program needn't handle non-finite values.
Results may differ from the reference program's by a relative error of at most 0.0099.
Values may be sent and summed in bfloat16 or wider, within the bound.
No kernel may reach another device: no remote copies, remote signals or barrier semaphores. Data moves between devices by JAX's collectives and lax.ppermute only.
A program may use at most 192 MiB of HBM per device.

```python
import jax
import jax.numpy as jnp
from jax import lax

D = 2048
HEADS = 32
HD = 64
RD = 32
FF = 8192
TOK_GRP = 512
SLOTS = 3
GROUPS = 8
TOKENS = 4096


def draw_lengths(key, part):
    subkeys = jax.random.split(key, 3)
    seq_counts = jax.random.randint(subkeys[0], (GROUPS,), 1, SLOTS + 1)
    single_group = jax.random.randint(subkeys[1], (), 0, GROUPS)
    seq_counts = jnp.where(jnp.arange(GROUPS) == single_group, 1, seq_counts)

    def cut_row(row_key, seq_count):
        cut_points = jax.random.permutation(row_key, TOK_GRP - 1)[:SLOTS - 1] + 1
        cut_points = jnp.where(jnp.arange(SLOTS - 1) < seq_count - 1, cut_points, TOK_GRP)
        cut_points = jnp.sort(cut_points.astype(jnp.int32))
        boundaries = jnp.concatenate([jnp.zeros((1,), jnp.int32), cut_points, jnp.full((1,), TOK_GRP, jnp.int32)])
        return (boundaries[1:] - boundaries[:-1]).astype(jnp.int32)
    return jax.vmap(cut_row)(jax.random.split(subkeys[2], GROUPS), seq_counts).astype(jnp.int32)


def draw_qkv_weight(key, part):
    entries = jax.random.normal(key, (D, 3, D), jnp.float32) * D ** (-0.5)
    return entries.astype(jnp.bfloat16)


def raised(values, key, source, target, parts, factor):
    def block_of(axis_at):
        return (jnp.arange(values.shape[axis_at]) // (values.shape[axis_at] // parts)).reshape((-1,) + (1,) * (values.ndim - 1 - axis_at))

    first = jax.random.permutation(key, parts)[block_of(target)]
    other_side = (block_of(target) + parts // 2) % parts
    return jnp.where((block_of(source) == first) | (block_of(source) == other_side), factor * values, values)


def block_levels(own_key, dims, cuts, least, largest):
    factor_of = 1.0
    for axis_at, shards_of in cuts:
        heights = jax.random.uniform(jax.random.fold_in(jax.random.fold_in(own_key, 6), axis_at), (shards_of,), jnp.float32, least / len(cuts), largest / len(cuts))
        factor_of = factor_of * jnp.repeat(jnp.exp(heights), dims[axis_at] // shards_of).reshape((-1,) + (1,) * (len(dims) - 1 - axis_at))
    return factor_of


def noise(rng, shape, scale, most, cuts=(), held_as=jnp.bfloat16):
    level = block_levels(rng, shape, cuts, -0.22, 0.18) if cuts else 1.0
    array = jax.random.normal(rng, shape, jnp.float32) * scale * level
    return jnp.minimum(jnp.maximum(array, -most), most).astype(held_as)


def gaussian_with(rng, shape, scale, most, cuts, heavy, kind=jnp.bfloat16):
    array = scale * jax.random.normal(rng, shape, jnp.float32)
    if cuts:
        array = array * block_levels(rng, shape, cuts, -0.22, 0.18)
    return jnp.clip(raised(array, jax.random.fold_in(rng, 3), *heavy), -most, most).astype(kind)


def setup_inputs(seed: int = 0) -> dict:
    streams_of = jax.random.split(jax.random.key(seed), 14)
    return {
        "hidden_in": noise(streams_of[0], (TOKENS, D), 1.0, 6.0, ((0, 32),)),
        "lengths": draw_lengths(jax.random.fold_in(streams_of[13], 71), 0),
        "norm_gain": jnp.clip(1.0 + 0.15 * jax.random.normal(streams_of[2], (D,), jnp.float32), 0.25, 1.75),
        "norm_shift": noise(streams_of[3], (D,), 0.5, 3.0, ((0, 32),), jnp.float32),
        "qkv_weight": draw_qkv_weight(jax.random.fold_in(streams_of[13], 71), 0),
        "qkv_bias": noise(streams_of[5], (3, HEADS, HD), 0.5, 3.0, ((1, 4), (2, 8))),
        "proj_weight": noise(streams_of[6], (D, D), (HD // 4) ** -0.5, 1.5, ((0, 4), (1, 8))),
        "proj_bias": noise(streams_of[7], (D,), 0.5, 3.0, ((0, 32),), jnp.float32),
        "up_weight": noise(streams_of[8], (D, FF), D ** -0.5, 0.125, ((0, 8), (1, 4))),
        "up_bias": noise(streams_of[9], (FF // 64, 64), 0.5, 3.0, ((0, 4), (1, 8))),
        "down_weight": noise(streams_of[10], (FF, D), FF ** -0.5, 0.0625, ((0, 4), (1, 8))),
        "down_bias": noise(streams_of[11], (D,), 0.5, 3.0, ((0, 32),), jnp.float32),
        "cotangent": gaussian_with(streams_of[12], (TOKENS, D), 1.0, 6.0, ((0, 32),), (0, 1, 32, 2.75)),
    }


@jax.custom_vjp
def low(v):
    return lax.optimization_barrier(v.astype(jnp.bfloat16)).astype(jnp.float32)

@jax.custom_vjp
def low_back(v):
    return v

def low_keep(v):
    return (low(v), None)

def low_pass(kept, grad):
    return (grad,)

def back_keep(v):
    return (v, None)

def back_low(kept, grad):
    return (low(grad),)
low.defvjp(low_keep, low_pass)
low_back.defvjp(back_keep, back_low)
epsilon = 1e-05
neg_large = -1e+30
highest = lax.Precision.HIGHEST

def gelu_tanh(values):
    return 0.5 * values * (1.0 + jnp.tanh(0.7978845608028654 * (values + 0.044715 * values * values * values)))

def rotary_tables(positions):
    half_rot = RD // 2
    frequency = jnp.exp(-jnp.log(10000.0) * (2.0 * jnp.arange(half_rot, dtype=jnp.float32) / RD))
    angles = positions.astype(jnp.float32)[:, None] * frequency[None, :]
    return (jnp.cos(angles)[:, None, :], jnp.sin(angles)[:, None, :])

def rotate(values, cosine, sine_table):
    half_rot = RD // 2
    front_half = values[..., :half_rot]
    back_half = values[..., half_rot:RD]
    return jnp.concatenate([front_half * cosine - back_half * sine_table, back_half * cosine + front_half * sine_table, values[..., RD:]], axis=-1)

def layout(lengths_row, rows_count):
    seq_ends = jnp.cumsum(lengths_row).astype(jnp.int32)
    row_index = jnp.arange(rows_count, dtype=jnp.int32)
    passed = row_index[:, None] >= seq_ends[None, :]
    sequence = lax.optimization_barrier(jnp.sum(passed.astype(jnp.int32), axis=1)).astype(jnp.int32)
    seq_start = lax.optimization_barrier(jnp.max(jnp.where(passed, seq_ends[None, :], 0), axis=1)).astype(jnp.int32)
    return (sequence, (row_index - seq_start).astype(jnp.int32))

def group_forward(rows_in, lengths_row, params):
    norm_gain, norm_shift, qkv_weight, qkv_bias, proj_weight, proj_bias, up_weight, up_bias, down_weight, down_bias = params
    centred = rows_in - lax.optimization_barrier(jnp.mean(rows_in, axis=1, keepdims=True))
    inv_scale = lax.rsqrt(lax.optimization_barrier(jnp.mean(centred * centred, axis=1, keepdims=True)) + epsilon)
    normed = low(centred * inv_scale * norm_gain + norm_shift)
    sequence, position = layout(lengths_row, TOK_GRP)
    cosine, sine_table = rotary_tables(position)
    qkv_rows = jnp.einsum('td,dce->tce', normed, qkv_weight, precision=highest) + qkv_bias.reshape(3, D)[None]
    qkv_rows = low_back(qkv_rows).reshape(TOK_GRP, 3, HEADS, HD)
    query = low(rotate(qkv_rows[:, 0], cosine, sine_table))
    keys_all = low(rotate(qkv_rows[:, 1], cosine, sine_table))
    values_all = low(qkv_rows[:, 2])
    row_ids = jnp.arange(TOK_GRP, dtype=jnp.int32)
    allowed = jnp.logical_and(sequence[:, None] == sequence[None, :], row_ids[None, :] <= row_ids[:, None])

    def attend_head(operands):
        query_head, key_head, value_head = operands
        scores = low_back(jnp.dot(query_head, key_head.T, precision=highest) * HD ** (-0.5))
        scores = jnp.where(allowed, scores, neg_large)
        row_max = lax.optimization_barrier(jnp.max(scores, axis=1, keepdims=True))
        weights = jnp.exp(scores - row_max)
        prob_rows = weights / lax.optimization_barrier(jnp.sum(weights, axis=1, keepdims=True))
        return jnp.dot(low(prob_rows), value_head, precision=highest)
    heads_out = lax.map(jax.checkpoint(attend_head), (query.transpose(1, 0, 2), keys_all.transpose(1, 0, 2), values_all.transpose(1, 0, 2)))
    attended = low_back(low(heads_out.transpose(1, 0, 2).reshape(TOK_GRP, D)))
    attn_branch = jnp.dot(attended, proj_weight, precision=highest)
    pre_act = low_back(jnp.dot(normed, up_weight, precision=highest) + up_bias.reshape(FF))
    activated = low(gelu_tanh(pre_act))
    mlp_branch = jnp.dot(activated, down_weight, precision=highest)
    return rows_in + attn_branch + proj_bias + mlp_branch + down_bias

def forward(inputs, lengths, params):
    grouped = inputs.reshape(GROUPS, TOK_GRP, D)
    group_step = jax.checkpoint(group_forward)

    def step(carry, operands):
        return (carry, group_step(operands[0], operands[1], params))
    unused, results = lax.scan(step, jnp.zeros((), jnp.float32), (grouped, lengths))
    return results.reshape(TOKENS, D)

def reference(hidden_in, lengths, norm_gain, norm_shift, qkv_weight, qkv_bias, proj_weight, proj_bias, up_weight, up_bias, down_weight, down_bias, cotangent):
    params = (norm_gain.astype(jnp.float32), norm_shift.astype(jnp.float32), qkv_weight.astype(jnp.float32), qkv_bias.astype(jnp.float32), proj_weight.astype(jnp.float32), proj_bias.astype(jnp.float32), up_weight.astype(jnp.float32), up_bias.astype(jnp.float32), down_weight.astype(jnp.float32), down_bias.astype(jnp.float32))
    outputs, pullback = jax.vjp(lambda inputs, weights: forward(inputs, lengths, weights), hidden_in.astype(jnp.float32), params)
    input_grad, weight_grads = pullback(cotangent.astype(jnp.float32))
    return (outputs.astype(jnp.bfloat16), input_grad, weight_grads[0], weight_grads[1], weight_grads[2], weight_grads[3], weight_grads[4], weight_grads[5], weight_grads[6], weight_grads[7], weight_grads[8], weight_grads[9])
```

```python
import jax
import jax.numpy as jnp
from jax import lax
from jax.sharding import Mesh, PartitionSpec as P

RD = 32
ZW = 4
XW = 2

epsilon = 1e-05
neg_large = -1e30
F32 = jnp.float32
BF = jnp.bfloat16


def gelu_tanh(values):
    return (
        0.5
        * values
        * (1.0 + jnp.tanh(0.7978845608028654 * (values + 0.044715 * values * values * values)))
    )


def rotary_tables(positions):
    half_rot = RD // 2
    frequency = jnp.exp(-jnp.log(10000.0) * (2.0 * jnp.arange(half_rot, dtype=F32) / RD))
    angles = positions.astype(F32)[:, None] * frequency[None, :]
    return (jnp.cos(angles)[:, None, :], jnp.sin(angles)[:, None, :])


def rotate(values, cosine, sine_table):
    half_rot = RD // 2
    front_half = values[..., :half_rot]
    back_half = values[..., half_rot:RD]
    return jnp.concatenate(
        [
            front_half * cosine - back_half * sine_table,
            back_half * cosine + front_half * sine_table,
            values[..., RD:],
        ],
        axis=-1,
    )


def make_body(sizes):
    nz, nr, nx, nc = (sizes[name] for name in ("z", "r", "x", "c"))

    def fetch(value, axis, step):
        n = sizes[axis]
        step %= n
        if step == 0:
            return value
        return lax.ppermute(value, axis, [((i + step) % n, i) for i in range(n)])

    def body(
        hidden_in,
        lengths,
        norm_gain,
        norm_shift,
        qkv_weight,
        qkv_bias,
        proj_weight,
        proj_bias,
        up_weight,
        up_bias,
        down_weight,
        down_bias,
        cotangent,
    ):
        zi, ri, xi, ci = (lax.axis_index(name) for name in ("z", "r", "x", "c"))
        n_dp, n_mp = nz * nr, nx * nc
        n_all = n_dp * n_mp
        rows, width = hidden_in.shape
        group_rows = rows * n_mp
        head_size = qkv_bias.shape[2] * n_dp
        heads = qkv_bias.shape[1] // nz
        hidden_units = up_weight.shape[1] // nz
        shard = norm_gain.shape[0]

        ub_rows = up_bias.shape[0] // nz
        small = jnp.concatenate(
            [
                norm_gain,
                norm_shift,
                proj_bias + down_bias,
                up_bias.astype(F32).reshape(-1),
                qkv_bias.astype(F32).reshape(-1),
                lengths.astype(F32).reshape(-1),
            ]
        )
        every = lax.all_to_all(
            jnp.broadcast_to(small[None], (n_all, small.shape[0])),
            ("z", "r", "x", "c"),
            0,
            0,
            tiled=True,
        )
        gain_full = every[:, :shard].reshape(width)
        shift_full = every[:, shard : 2 * shard].reshape(width)
        bias_full = every[:, 2 * shard : 3 * shard].reshape(width)
        mp_at = xi * nc + ci
        mine = lax.dynamic_index_in_dim(
            every.reshape(n_dp, n_mp, -1), mp_at, axis=1, keepdims=False
        )
        at = 3 * shard
        ub_all = mine[:, at : at + up_bias.size].reshape(n_dp, up_bias.shape[0], up_bias.shape[1])
        ub_all = lax.dynamic_slice_in_dim(ub_all, zi * ub_rows, ub_rows, axis=1)
        ub_all = ub_all.transpose(1, 0, 2).reshape(hidden_units)
        at += up_bias.size
        qb_all = mine[:, at : at + qkv_bias.size].reshape((n_dp,) + qkv_bias.shape)
        qb_all = lax.dynamic_slice_in_dim(qb_all, zi * heads, heads, axis=2)
        qb_all = qb_all.transpose(1, 2, 0, 3).reshape(3, heads, head_size)
        at += qkv_bias.size
        group_lengths = mine[:, at:].astype(jnp.int32).reshape(nz, nr, -1)
        group_lengths = lax.dynamic_index_in_dim(group_lengths, ri, axis=1, keepdims=False)

        def gather_rows(own):
            groups = []
            for dz in range(nz):
                here = fetch(own, "z", dz)
                line = [fetch(here, "x", dx) for dx in range(nx)]
                groups.append(
                    jnp.concatenate([fetch(part, "c", dc) for dc in range(nc) for part in line])
                )
            return jnp.concatenate(groups)

        def gather_weight(block, cut, width_axis):
            size = block.shape[cut] // nz
            shape = list(block.shape)
            shape[cut] = size
            step = shape[width_axis]
            shape[width_axis] = step * n_dp
            whole = jnp.zeros(shape, block.dtype)
            for dz in range(nz):
                to = (zi + nz - dz) % nz
                part = lax.dynamic_slice_in_dim(block, to * size, size, axis=cut)
                part = fetch(part, "z", dz)
                for dr in range(nr):
                    at = (((zi + dz) % nz) * nr + (ri + dr) % nr) * step
                    whole = lax.dynamic_update_slice_in_dim(
                        whole, fetch(part, "r", dr), at, axis=width_axis
                    )
            return whole

        hidden_plane = gather_rows(hidden_in)
        qkv_all = gather_weight(qkv_weight, 2, 0)
        up_all = gather_weight(up_weight, 1, 0)
        grad_plane = gather_rows(cotangent)
        down_all = gather_weight(down_weight, 0, 1)
        proj_all = gather_weight(proj_weight, 0, 1)
        tokens = hidden_plane.shape[0]

        def standardize(rows_in):
            centred = rows_in - jnp.mean(rows_in, axis=1, keepdims=True)
            inv_scale = lax.rsqrt(jnp.mean(centred * centred, axis=1, keepdims=True) + epsilon)
            return centred * inv_scale, inv_scale

        normed = (standardize(hidden_plane.astype(F32))[0] * gain_full + shift_full).astype(BF)

        local = jnp.arange(group_rows, dtype=jnp.int32)
        dc, dx, row = local // (nx * rows), (local // rows) % nx, local % rows
        row_ids = (((xi + dx) % nx) * nc + (ci + dc) % nc) * rows + row
        relative = (zi + jnp.arange(nz)) % nz
        seq_ends = jnp.cumsum(group_lengths, axis=1)[relative]
        passed = row_ids[None, :, None] >= seq_ends[:, None, :]
        sequence = jnp.sum(passed.astype(jnp.int32), axis=2)
        position = row_ids[None] - jnp.max(jnp.where(passed, seq_ends[:, None, :], 0), axis=2)
        cosine, sine_table = rotary_tables(position.reshape(-1))
        allowed = jnp.logical_and(
            sequence[:, :, None] == sequence[:, None, :],
            (row_ids[None, :] <= row_ids[:, None])[None],
        )[:, None]

        contract_rows = (((0,), (0,)), ((), ()))
        contract_cols = (((1,), (1,)), ((), ()))
        score_scale = head_size ** (-0.5)
        qkv_flat = qkv_all.reshape(width, 3 * heads * head_size)
        qkv_rows = jnp.dot(normed, qkv_flat, preferred_element_type=F32) + qb_all.reshape(-1)
        qkv_rows = qkv_rows.reshape(tokens, 3, heads, head_size)
        grouped = (nz, group_rows, heads, head_size)
        query_bf = rotate(qkv_rows[:, 0], cosine, sine_table).astype(BF).reshape(grouped)
        key_bf = rotate(qkv_rows[:, 1], cosine, sine_table).astype(BF).reshape(grouped)
        value_bf = qkv_rows[:, 2].astype(BF).reshape(grouped)

        scores = (
            jnp.einsum("gqhd,gkhd->ghqk", query_bf, key_bf, preferred_element_type=F32)
            * score_scale
        )
        scores = jnp.where(allowed, scores, neg_large)
        row_max = jnp.max(scores, axis=3, keepdims=True)
        weights = jnp.exp(scores - row_max)
        prob_rows = weights / jnp.sum(weights, axis=3, keepdims=True)
        prob_bf = prob_rows.astype(BF)
        attended = jnp.einsum("ghqk,gkhd->gqhd", prob_bf, value_bf, preferred_element_type=F32)
        attended = attended.astype(BF).reshape(tokens, heads * head_size)

        pre_act = jnp.dot(normed, up_all, preferred_element_type=F32) + ub_all
        activated, gelu_pull = jax.vjp(gelu_tanh, pre_act)
        activated = activated.astype(BF)

        def scatter_rows(part):
            part = part.reshape(nz, nc, nx * rows, width)
            total = None
            for dz in reversed(range(nz)):
                piece = part[dz, 0]
                for dc in range(1, nc):
                    piece = piece + fetch(part[dz, dc].astype(BF), "c", -dc).astype(F32)
                piece = piece.reshape(nx, rows, width)
                line = piece[0]
                for dx in range(1, nx):
                    line = line + fetch(piece[dx].astype(BF), "x", -dx).astype(F32)
                line = fetch(line.astype(BF), "z", -dz).astype(F32) if dz else line
                total = line if total is None else total + line
            return total

        def scatter_weight(grad, cut, width_axis):
            size = grad.shape[cut]
            step = grad.shape[width_axis] // n_dp
            shape = list(grad.shape)
            shape[width_axis] = step
            shape[cut] = size * nz
            out = jnp.zeros(shape, F32)
            for dz in range(nz):
                to = (zi + dz) % nz

                def block(dr):
                    at = (to * nr + (ri + dr) % nr) * step
                    return lax.dynamic_slice_in_dim(grad, at, step, axis=width_axis)

                piece = block(0)
                for dr in range(1, nr):
                    piece = piece + fetch(block(dr).astype(BF), "r", -dr).astype(F32)
                if dz:
                    piece = fetch(piece.astype(BF), "z", -dz).astype(F32)
                out = lax.dynamic_update_slice_in_dim(
                    out, piece, ((zi + nz - dz) % nz) * size, axis=cut
                )
            return out

        grad_act = lax.dot_general(
            grad_plane, down_all, contract_cols, preferred_element_type=F32
        )
        grad_pre = gelu_pull(grad_act)[0].astype(BF)
        down_grad = lax.dot_general(
            activated, grad_plane, contract_rows, preferred_element_type=F32
        )
        down_out = scatter_weight(down_grad, 0, 1)
        up_grad = lax.dot_general(normed, grad_pre, contract_rows, preferred_element_type=F32)
        up_out = scatter_weight(up_grad, 1, 0)
        grad_heads = lax.dot_general(
            grad_plane, proj_all, contract_cols, preferred_element_type=F32
        ).astype(BF)
        proj_grad = lax.dot_general(attended, grad_plane, contract_rows, preferred_element_type=F32)
        proj_out = scatter_weight(proj_grad, 0, 1)

        grad_heads = grad_heads.reshape(grouped)
        grad_probs = jnp.einsum(
            "gqhd,gkhd->ghqk", grad_heads, value_bf, preferred_element_type=F32
        )
        row_delta = jnp.sum(prob_rows * grad_probs, axis=3, keepdims=True)
        grad_scores = (prob_rows * (grad_probs - row_delta)).astype(BF)
        grad_query = (
            jnp.einsum("ghqk,gkhd->gqhd", grad_scores, key_bf, preferred_element_type=F32)
            * score_scale
        )
        grad_key = (
            jnp.einsum("ghqk,gqhd->gkhd", grad_scores, query_bf, preferred_element_type=F32)
            * score_scale
        )
        grad_value = jnp.einsum("ghqk,gqhd->gkhd", prob_bf, grad_heads, preferred_element_type=F32)
        flat = (tokens, heads, head_size)
        grad_qkv = jnp.stack(
            [
                rotate(grad_query.reshape(flat), cosine, -sine_table),
                rotate(grad_key.reshape(flat), cosine, -sine_table),
                grad_value.reshape(flat),
            ],
            axis=1,
        )
        grad_qkv = grad_qkv.astype(BF).reshape(tokens, 3 * heads * head_size)
        grad_normed = lax.dot_general(
            grad_pre, up_all, contract_cols, preferred_element_type=F32
        ) + lax.dot_general(grad_qkv, qkv_flat, contract_cols, preferred_element_type=F32)
        grad_local = scatter_rows(grad_normed)
        qkv_grad = lax.dot_general(normed, grad_qkv, contract_rows, preferred_element_type=F32)
        qkv_out = scatter_weight(qkv_grad.reshape(width, 3, heads * head_size), 2, 0)

        branch_part = jnp.dot(attended, proj_all, preferred_element_type=F32) + jnp.dot(
            activated, down_all, preferred_element_type=F32
        )
        branch_sum = scatter_rows(branch_part)
        inputs32 = hidden_in.astype(F32)
        layer_out = (inputs32 + branch_sum + bias_full).astype(BF)

        col_sums = jnp.concatenate(
            [
                jnp.sum(grad_pre.astype(F32), axis=0).reshape(ub_rows, head_size),
                jnp.sum(grad_qkv.astype(F32), axis=0).reshape(3 * heads, head_size),
            ]
        )
        bias_rows = scatter_weight_small(col_sums, zi, ri, fetch, nz, nr)
        ubias_out = bias_rows[:, :ub_rows].reshape(nz * ub_rows, -1)
        qbias_out = bias_rows[:, ub_rows:].reshape(nz, 3, heads, -1)
        qbias_out = qbias_out.transpose(1, 0, 2, 3).reshape(3, nz * heads, -1)

        shard_at = ((zi * nr + ri) * nx + xi) * nc + ci
        row_sums = jnp.sum(grad_plane.astype(F32), axis=0)

        def shard_of(dr):
            at = ((zi * nr + (ri + dr) % nr) * nx + xi) * nc + ci
            return lax.dynamic_slice_in_dim(row_sums, at * shard, shard)

        bias_out = shard_of(0)
        for dr in range(1, nr):
            bias_out = bias_out + fetch(shard_of(dr), "r", -dr)

        standard, inv_scale = standardize(inputs32)
        sums = jnp.stack([jnp.sum(grad_local * standard, axis=0), jnp.sum(grad_local, axis=0)])
        sums = sums.reshape(2, n_all, shard).transpose(1, 0, 2).reshape(n_all, 2 * shard)
        sums = lax.all_to_all(sums, ("z", "r", "x", "c"), 0, 0, tiled=True)
        sums = jnp.sum(sums, axis=0)
        gain_out, shift_out = sums[:shard], sums[shard:]
        grad_unit = grad_local * gain_full
        input_grad = cotangent.astype(F32) + inv_scale * (
            grad_unit
            - jnp.mean(grad_unit, axis=1, keepdims=True)
            - standard * jnp.mean(grad_unit * standard, axis=1, keepdims=True)
        )
        return (
            layer_out,
            input_grad,
            gain_out,
            shift_out,
            qkv_out,
            qbias_out,
            proj_out,
            bias_out,
            up_out,
            ubias_out,
            down_out,
            bias_out,
        )

    return body


def scatter_weight_small(sums, zi, ri, fetch, nz, nr):
    count, cols = sums.shape
    blocks = sums.reshape(count, nz, nr, cols // (nz * nr)).transpose(1, 2, 0, 3)
    total = lax.dynamic_index_in_dim(blocks, ri, axis=1, keepdims=False)
    for dr in range(1, nr):
        other = lax.dynamic_index_in_dim(blocks, (ri + dr) % nr, axis=1, keepdims=False)
        total = total + fetch(other, "r", -dr)
    out = jnp.zeros((nz, count, cols // (nz * nr)), F32)
    for dz in range(nz):
        piece = lax.dynamic_index_in_dim(total, (zi + dz) % nz, axis=0)
        out = lax.dynamic_update_slice_in_dim(
            out, fetch(piece, "z", -dz), (zi + nz - dz) % nz, axis=0
        )
    return out


def solution(mesh):
    n_dp, n_mp = mesh.shape["dp"], mesh.shape["mp"]
    sizes = {"z": ZW, "r": n_dp // ZW, "x": XW, "c": n_mp // XW}
    fine = Mesh(mesh.devices.reshape(tuple(sizes.values())), tuple(sizes))
    dp, mp = ("z", "r"), ("x", "c")
    every = dp + mp
    rows, vector = P(every, None), P(every)
    in_specs = (
        rows,
        P(dp, None),
        vector,
        vector,
        P(dp, None, mp),
        P(None, mp, dp),
        P(mp, dp),
        vector,
        P(dp, mp),
        P(mp, dp),
        P(mp, dp),
        vector,
        rows,
    )
    out_specs = (
        rows,
        rows,
        vector,
        vector,
        P(dp, None, mp),
        P(None, mp, dp),
        P(mp, dp),
        vector,
        P(dp, mp),
        P(mp, dp),
        P(mp, dp),
        vector,
    )
    return jax.shard_map(
        make_body(sizes), mesh=fine, in_specs=in_specs, out_specs=out_specs, check_vma=False
    )
```

```python
import jax
import jax.numpy as jnp
from jax import lax
from jax.sharding import Mesh, PartitionSpec as P

RD = 32
ZW = 4
XW = 2

epsilon = 1e-05
neg_large = -1e30
F32 = jnp.float32
BF = jnp.bfloat16


def gelu_tanh(values):
    return (
        0.5
        * values
        * (1.0 + jnp.tanh(0.7978845608028654 * (values + 0.044715 * values * values * values)))
    )


def rotary_tables(positions):
    half_rot = RD // 2
    frequency = jnp.exp(-jnp.log(10000.0) * (2.0 * jnp.arange(half_rot, dtype=F32) / RD))
    angles = positions.astype(F32)[:, None] * frequency[None, :]
    return (jnp.cos(angles)[:, None, :], jnp.sin(angles)[:, None, :])


def rotate(values, cosine, sine_table):
    half_rot = RD // 2
    front_half = values[..., :half_rot]
    back_half = values[..., half_rot:RD]
    return jnp.concatenate(
        [
            front_half * cosine - back_half * sine_table,
            back_half * cosine + front_half * sine_table,
            values[..., RD:],
        ],
        axis=-1,
    )


def make_body(sizes):
    nz, nr, nx, nc = (sizes[name] for name in ("z", "r", "x", "c"))

    def fetch(value, axis, step):
        n = sizes[axis]
        step %= n
        if step == 0:
            return value
        return lax.ppermute(value, axis, [((i + step) % n, i) for i in range(n)])

    def body(
        hidden_in,
        lengths,
        norm_gain,
        norm_shift,
        qkv_weight,
        qkv_bias,
        proj_weight,
        proj_bias,
        up_weight,
        up_bias,
        down_weight,
        down_bias,
        cotangent,
    ):
        zi, ri, xi, ci = (lax.axis_index(name) for name in ("z", "r", "x", "c"))
        n_dp, n_mp = nz * nr, nx * nc
        n_all = n_dp * n_mp
        rows, width = hidden_in.shape
        group_rows = rows * n_mp
        head_size = qkv_bias.shape[2] * n_dp
        heads = qkv_bias.shape[1] // nz
        hidden_units = up_weight.shape[1] // nz
        shard = norm_gain.shape[0]

        def to_plane(value):
            lead = value.shape[:-1]
            value = value.reshape(lead + (nz, nr, -1))
            value = jnp.moveaxis(value, -2, len(lead))
            value = jnp.concatenate([value, value], axis=len(lead))
            value = lax.dynamic_slice_in_dim(value, ri, nr, axis=len(lead))
            return value.reshape(lead + (width,))

        def from_plane(value):
            lead = value.shape[:-1]
            value = value.reshape(lead + (nr, nz, -1))
            value = jnp.concatenate([value, value], axis=len(lead))
            value = lax.dynamic_slice_in_dim(value, nr - ri, nr, axis=len(lead))
            return jnp.moveaxis(value, len(lead), -2).reshape(lead + (width,))

        def exchange(value, axes):
            return lax.all_to_all(value, axes, 0, 0, tiled=True)

        ub_rows = up_bias.shape[0] // nz
        small = jnp.concatenate(
            [
                norm_gain,
                norm_shift,
                proj_bias + down_bias,
                up_bias.astype(F32).reshape(-1),
                qkv_bias.astype(F32).reshape(-1),
                lengths.astype(F32).reshape(-1),
            ]
        )
        every = exchange(
            jnp.broadcast_to(small[None], (n_all, small.shape[0])), ("z", "r", "x", "c")
        )
        gain_full = to_plane(every[:, :shard].reshape(width))
        shift_full = to_plane(every[:, shard : 2 * shard].reshape(width))
        bias_full = to_plane(every[:, 2 * shard : 3 * shard].reshape(width))
        mine = lax.dynamic_index_in_dim(
            every.reshape(n_dp, n_mp, -1), xi * nc + ci, axis=1, keepdims=False
        )
        at = 3 * shard
        ub_all = mine[:, at : at + up_bias.size].reshape(n_dp, up_bias.shape[0], up_bias.shape[1])
        ub_all = lax.dynamic_slice_in_dim(ub_all, zi * ub_rows, ub_rows, axis=1)
        ub_all = ub_all.transpose(1, 0, 2).reshape(hidden_units)
        at += up_bias.size
        qb_all = mine[:, at : at + qkv_bias.size].reshape((n_dp,) + qkv_bias.shape)
        qb_all = lax.dynamic_slice_in_dim(qb_all, zi * heads, heads, axis=2)
        qb_all = qb_all.transpose(1, 2, 0, 3).reshape(3 * heads * head_size)
        at += qkv_bias.size
        group_lengths = mine[:, at:].astype(jnp.int32).reshape(nz, nr, -1)
        group_lengths = lax.dynamic_index_in_dim(group_lengths, ri, axis=1, keepdims=False)

        def gather_rows(own):
            own = to_plane(own)
            here = exchange(jnp.broadcast_to(own[None], (nz, rows, width)), "z")
            here = here.reshape(nz * rows, width)
            line = [fetch(here, "x", dx) for dx in range(nx)]
            return jnp.concatenate([fetch(part, "c", dc) for dc in range(nc) for part in line])

        def gather_weight(blocks):
            own = exchange(blocks, "z")
            return [fetch(own, "r", dr) for dr in range(nr)]

        step = width // n_dp
        units = heads * head_size
        hidden_plane = gather_rows(hidden_in)
        tokens = hidden_plane.shape[0]
        qkv_all = gather_weight(
            qkv_weight.reshape(step, 3, nz, units).transpose(2, 0, 1, 3).reshape(nz, step, 3 * units)
        )
        qkv_all = jnp.concatenate(qkv_all).reshape(width, 3 * units)
        grad_plane = gather_rows(cotangent)
        up_all = gather_weight(up_weight.reshape(step, nz, hidden_units).transpose(1, 0, 2))
        up_all = jnp.concatenate(up_all).reshape(width, hidden_units)
        down_all = gather_weight(down_weight.reshape(nz, hidden_units, step))
        down_all = jnp.concatenate(down_all).transpose(1, 0, 2).reshape(hidden_units, width)
        proj_all = gather_weight(proj_weight.reshape(nz, units, step))
        proj_all = jnp.concatenate(proj_all).transpose(1, 0, 2).reshape(units, width)

        def standardize(rows_in):
            centred = rows_in - jnp.mean(rows_in, axis=1, keepdims=True)
            inv_scale = lax.rsqrt(jnp.mean(centred * centred, axis=1, keepdims=True) + epsilon)
            return centred * inv_scale, inv_scale

        normed = (standardize(hidden_plane.astype(F32))[0] * gain_full + shift_full).astype(BF)

        local = jnp.arange(n_mp * rows, dtype=jnp.int32)
        dc, dx, row = local // (nx * rows), (local // rows) % nx, local % rows
        row_ids = (((xi + dx) % nx) * nc + (ci + dc) % nc) * rows + row
        seq_ends = jnp.cumsum(group_lengths, axis=1)
        passed = row_ids[None, :, None] >= seq_ends[:, None, :]
        sequence = jnp.sum(passed.astype(jnp.int32), axis=2)
        position = row_ids[None] - jnp.max(jnp.where(passed, seq_ends[:, None, :], 0), axis=2)
        cosine, sine_table = rotary_tables(position.reshape(-1))
        allowed = jnp.logical_and(
            sequence[:, :, None] == sequence[:, None, :],
            (row_ids[None, :] <= row_ids[:, None])[None],
        )[:, None]

        def by_group(value):
            value = value.reshape((n_mp, nz, rows) + value.shape[1:])
            return value.transpose(1, 0, 2, *range(3, value.ndim)).reshape(
                (nz * n_mp * rows,) + value.shape[3:]
            )

        def by_row(value):
            value = value.reshape((nz, n_mp, rows) + value.shape[1:])
            return value.transpose(1, 0, 2, *range(3, value.ndim)).reshape(
                (nz * n_mp * rows,) + value.shape[3:]
            )

        contract_rows = (((0,), (0,)), ((), ()))
        contract_cols = (((1,), (1,)), ((), ()))
        score_scale = head_size ** (-0.5)
        qkv_rows = jnp.dot(normed, qkv_all, preferred_element_type=F32) + qb_all
        qkv_rows = by_group(qkv_rows).reshape(tokens, 3, heads, head_size)
        grouped = (nz, group_rows, heads, head_size)
        query_bf = rotate(qkv_rows[:, 0], cosine, sine_table).astype(BF).reshape(grouped)
        key_bf = rotate(qkv_rows[:, 1], cosine, sine_table).astype(BF).reshape(grouped)
        value_bf = qkv_rows[:, 2].astype(BF).reshape(grouped)

        scores = (
            jnp.einsum("gqhd,gkhd->ghqk", query_bf, key_bf, preferred_element_type=F32)
            * score_scale
        )
        scores = jnp.where(allowed, scores, neg_large)
        row_max = jnp.max(scores, axis=3, keepdims=True)
        weights = jnp.exp(scores - row_max)
        prob_rows = weights / jnp.sum(weights, axis=3, keepdims=True)
        prob_bf = prob_rows.astype(BF)
        attended = jnp.einsum("ghqk,gkhd->gqhd", prob_bf, value_bf, preferred_element_type=F32)
        attended = by_row(attended.astype(BF).reshape(tokens, units))

        pre_act = jnp.dot(normed, up_all, preferred_element_type=F32) + ub_all
        activated, gelu_pull = jax.vjp(gelu_tanh, pre_act)
        activated = activated.astype(BF)

        def scatter_rows(part):
            part = part.reshape(nc, tokens // nc, width)
            piece = part[0]
            for dc in range(1, nc):
                piece = piece + fetch(part[dc].astype(BF), "c", -dc).astype(F32)
            piece = piece.reshape(nx, nz * rows, width)
            line = piece[0]
            for dx in range(1, nx):
                line = line + fetch(piece[dx].astype(BF), "x", -dx).astype(F32)
            line = exchange(line.astype(BF).reshape(nz, rows, width), "z")
            return jnp.sum(line.astype(F32), axis=0)

        def scatter_weight(grad):
            piece = grad[0]
            for dr in range(1, nr):
                piece = piece + fetch(grad[dr].astype(BF), "r", -dr).astype(F32)
            return exchange(piece.astype(BF), "z").astype(F32)

        grad_act = lax.dot_general(
            grad_plane, down_all, contract_cols, preferred_element_type=F32
        )
        grad_pre = gelu_pull(grad_act)[0].astype(BF)
        down_grad = lax.dot_general(
            activated, grad_plane, contract_rows, preferred_element_type=F32
        )
        down_out = scatter_weight(
            down_grad.reshape(hidden_units, nr, nz, step).transpose(1, 2, 0, 3)
        ).reshape(nz * hidden_units, step)
        up_grad = lax.dot_general(normed, grad_pre, contract_rows, preferred_element_type=F32)
        up_out = scatter_weight(up_grad.reshape(nr, nz, step, hidden_units))
        up_out = up_out.transpose(1, 0, 2).reshape(step, nz * hidden_units)
        grad_heads = lax.dot_general(
            grad_plane, proj_all, contract_cols, preferred_element_type=F32
        ).astype(BF)
        proj_grad = lax.dot_general(attended, grad_plane, contract_rows, preferred_element_type=F32)
        proj_out = scatter_weight(
            proj_grad.reshape(units, nr, nz, step).transpose(1, 2, 0, 3)
        ).reshape(nz * units, step)

        grad_heads = by_group(grad_heads).reshape(grouped)
        grad_probs = jnp.einsum(
            "gqhd,gkhd->ghqk", grad_heads, value_bf, preferred_element_type=F32
        )
        row_delta = jnp.sum(prob_rows * grad_probs, axis=3, keepdims=True)
        grad_scores = (prob_rows * (grad_probs - row_delta)).astype(BF)
        grad_query = (
            jnp.einsum("ghqk,gkhd->gqhd", grad_scores, key_bf, preferred_element_type=F32)
            * score_scale
        )
        grad_key = (
            jnp.einsum("ghqk,gqhd->gkhd", grad_scores, query_bf, preferred_element_type=F32)
            * score_scale
        )
        grad_value = jnp.einsum("ghqk,gqhd->gkhd", prob_bf, grad_heads, preferred_element_type=F32)
        flat = (tokens, heads, head_size)
        grad_qkv = jnp.stack(
            [
                rotate(grad_query.reshape(flat), cosine, -sine_table),
                rotate(grad_key.reshape(flat), cosine, -sine_table),
                grad_value.reshape(flat),
            ],
            axis=1,
        )
        grad_qkv = by_row(grad_qkv.astype(BF).reshape(tokens, 3 * units))
        grad_normed = lax.dot_general(
            grad_pre, up_all, contract_cols, preferred_element_type=F32
        ) + lax.dot_general(grad_qkv, qkv_all, contract_cols, preferred_element_type=F32)
        grad_local = scatter_rows(grad_normed)
        qkv_grad = lax.dot_general(normed, grad_qkv, contract_rows, preferred_element_type=F32)
        qkv_out = scatter_weight(qkv_grad.reshape(nr, nz, step, 3 * units))
        qkv_out = qkv_out.reshape(nz, step, 3, units).transpose(1, 2, 0, 3)
        qkv_out = qkv_out.reshape(step, 3, nz * units)

        branch_part = jnp.dot(attended, proj_all, preferred_element_type=F32) + jnp.dot(
            activated, down_all, preferred_element_type=F32
        )
        branch_sum = scatter_rows(branch_part)
        layer_out = from_plane(branch_sum + bias_full)
        inputs32 = hidden_in.astype(F32)
        layer_out = (inputs32 + layer_out).astype(BF)

        col_sums = jnp.concatenate(
            [
                jnp.sum(grad_pre.astype(F32), axis=0).reshape(ub_rows, head_size),
                jnp.sum(grad_qkv.astype(F32), axis=0).reshape(3 * heads, head_size),
            ]
        )
        count = ub_rows + 3 * heads
        block = head_size // n_dp
        col_sums = col_sums.reshape(count, n_dp, block).transpose(1, 0, 2).reshape(n_dp, -1)
        row_sums = from_plane(jnp.sum(grad_plane.astype(F32), axis=0))
        row_sums = lax.dynamic_index_in_dim(
            row_sums.reshape(n_dp, n_mp, shard), xi * nc + ci, axis=1, keepdims=False
        )
        sums = exchange(jnp.concatenate([col_sums, row_sums], axis=1), ("z", "r"))
        sums = jnp.sum(sums.reshape(nz, nr, -1), axis=1)
        bias_out = sums[0, count * block :]
        bias_rows = sums[:, : count * block].reshape(nz, count, block)
        ubias_out = bias_rows[:, :ub_rows].reshape(nz * ub_rows, block)
        qbias_out = bias_rows[:, ub_rows:].reshape(nz, 3, heads, block)
        qbias_out = qbias_out.transpose(1, 0, 2, 3).reshape(3, nz * heads, block)

        standard, inv_scale = standardize(to_plane(hidden_in).astype(F32))
        sums = jnp.stack([jnp.sum(grad_local * standard, axis=0), jnp.sum(grad_local, axis=0)])
        sums = from_plane(sums).reshape(2, n_all, shard).transpose(1, 0, 2)
        sums = exchange(sums.reshape(n_all, 2 * shard), ("z", "r", "x", "c"))
        sums = jnp.sum(sums, axis=0)
        gain_out, shift_out = sums[:shard], sums[shard:]
        grad_unit = grad_local * gain_full
        input_grad = inv_scale * (
            grad_unit
            - jnp.mean(grad_unit, axis=1, keepdims=True)
            - standard * jnp.mean(grad_unit * standard, axis=1, keepdims=True)
        )
        input_grad = cotangent.astype(F32) + from_plane(input_grad)
        return (
            layer_out,
            input_grad,
            gain_out,
            shift_out,
            qkv_out,
            qbias_out,
            proj_out,
            bias_out,
            up_out,
            ubias_out,
            down_out,
            bias_out,
        )

    return body


def solution(mesh):
    n_dp, n_mp = mesh.shape["dp"], mesh.shape["mp"]
    sizes = {"z": ZW, "r": n_dp // ZW, "x": XW, "c": n_mp // XW}
    fine = Mesh(mesh.devices.reshape(tuple(sizes.values())), tuple(sizes))
    dp, mp = ("z", "r"), ("x", "c")
    every = dp + mp
    rows, vector = P(every, None), P(every)
    in_specs = (
        rows,
        P(dp, None),
        vector,
        vector,
        P(dp, None, mp),
        P(None, mp, dp),
        P(mp, dp),
        vector,
        P(dp, mp),
        P(mp, dp),
        P(mp, dp),
        vector,
        rows,
    )
    out_specs = (
        rows,
        rows,
        vector,
        vector,
        P(dp, None, mp),
        P(None, mp, dp),
        P(mp, dp),
        vector,
        P(dp, mp),
        P(mp, dp),
        P(mp, dp),
        vector,
    )
    return jax.shard_map(
        make_body(sizes), mesh=fine, in_specs=in_specs, out_specs=out_specs, check_vma=False
    )
```

```python
import functools

import jax
import jax.numpy as jnp
from jax import lax
from jax.experimental import pallas as pl
from jax.experimental.pallas import tpu as pltpu
from jax.sharding import Mesh, PartitionSpec as P

RD = 32
ZW = 4
XW = 2

epsilon = 1e-05
neg_large = -1e30
F32 = jnp.float32
BF = jnp.bfloat16
NN = (((1,), (0,)), ((), ()))
NT = (((1,), (1,)), ((), ()))
TN = (((0,), (0,)), ((), ()))


def matmul(lhs, rhs, dims):
    return lax.dot_general(lhs, rhs, dims, preferred_element_type=F32)


def gelu_and_slope(values):
    cube = values * values * values
    bent = jnp.tanh(0.7978845608028654 * (values + 0.044715 * cube))
    inner = 0.7978845608028654 * (1.0 + 3.0 * 0.044715 * values * values)
    gelu = 0.5 * values * (1.0 + bent)
    slope = 0.5 * (1.0 + bent) + 0.5 * values * (1.0 - bent * bent) * inner
    return gelu, slope


def standardize(rows_in):
    centred = rows_in - jnp.mean(rows_in, axis=1, keepdims=True)
    inv_scale = lax.rsqrt(jnp.mean(centred * centred, axis=1, keepdims=True) + epsilon)
    return centred * inv_scale, inv_scale


def rotary_tables(positions):
    half_rot = RD // 2
    frequency = jnp.exp(-jnp.log(10000.0) * (2.0 * jnp.arange(half_rot, dtype=F32) / RD))
    angles = positions.astype(F32)[..., None] * frequency
    return jnp.cos(angles), jnp.sin(angles)


def whole_spec(value):
    zeros = (0,) * value.ndim
    return pl.BlockSpec(value.shape, lambda *_: zeros)


def rows_spec(n_mp, rows, cols):
    return pl.BlockSpec((n_mp, 1, rows, cols), lambda g, *_: (0, g, 0, 0))


def slot_spec(n_mp, rows, cols):
    return pl.BlockSpec((n_mp, 1, rows, cols), lambda _, slot: (0, slot[0], 0, 0))


def flat_rows(ref):
    n_mp, _, rows, cols = ref.shape
    return ref[...].reshape(n_mp * rows, cols)


def put_rows(ref, value):
    ref[...] = value.astype(ref.dtype).reshape(ref.shape)


def cost(flops, bytes_accessed):
    return pl.CostEstimate(flops=int(flops), bytes_accessed=int(bytes_accessed), transcendentals=0)


def norm_group(slot, pieces, gain, shift, before, nz, nr):
    n_mp = len(pieces)
    rows, width = pieces[0].shape
    part = width // nr
    shape = jax.ShapeDtypeStruct((n_mp, nz, rows, part), BF)

    def kernel(slot_ref, *refs):
        ins, gain_ref, shift_ref = refs[:n_mp], refs[n_mp], refs[n_mp + 1]
        outs = refs[-nr:]
        for at in range(n_mp):
            unit, _ = standardize(ins[at][...].astype(F32))
            normed = (unit * gain_ref[...] + shift_ref[...]).astype(BF)
            for r in range(nr):
                outs[r][at, 0] = normed[:, r * part : (r + 1) * part]

    before = before or []
    operands = list(pieces) + [gain, shift]
    return pl.pallas_call(
        kernel,
        out_shape=[shape] * nr,
        grid_spec=pltpu.PrefetchScalarGridSpec(
            num_scalar_prefetch=1,
            grid=(1,),
            in_specs=[whole_spec(v) for v in operands]
            + [pl.BlockSpec(memory_space=pl.ANY)] * len(before),
            out_specs=[slot_spec(n_mp, rows, part)] * nr,
        ),
        input_output_aliases={1 + len(operands) + k: k for k in range(len(before))},
        cost_estimate=cost(10 * n_mp * rows * width, 4 * n_mp * rows * width),
        name="norm",
    )(slot, *operands, *before)


def project(parts, blocks, bias, gelu):
    n_mp, nz, rows, part = parts[0].shape
    cols = blocks[0].shape[1]
    nr = len(parts)

    def kernel(*refs):
        total = refs[2 * nr][...]
        for r in range(nr):
            total = total + matmul(flat_rows(refs[r]), refs[nr + r][...], NN)
        outs = refs[2 * nr + 1 :]
        if gelu:
            act, slope = gelu_and_slope(total)
            put_rows(outs[0], act)
            put_rows(outs[1], slope)
        else:
            put_rows(outs[0], total)

    full = (n_mp, nz, rows, cols)
    spec = rows_spec(n_mp, rows, cols)
    kinds = (BF, F32) if gelu else (F32,)
    return pl.pallas_call(
        kernel,
        out_shape=[jax.ShapeDtypeStruct(full, kind) for kind in kinds],
        grid=(nz,),
        in_specs=[rows_spec(n_mp, rows, part)] * nr
        + [whole_spec(v) for v in blocks]
        + [whole_spec(bias)],
        out_specs=[spec] * len(kinds),
        cost_estimate=cost(2 * n_mp * nz * rows * part * nr * cols, 2 * n_mp * nz * rows * part * nr),
        name="project",
    )(*parts, *blocks, bias)


def back_group(slot, pieces, slope, down, proj, before):
    n_mp, nz, rows, hidden = slope.shape
    width = pieces[0].shape[1]
    nr = len(down)
    part = width // nr
    units = proj[0].shape[1]
    shapes = [(part, BF)] * nr + [(hidden, BF), (units, BF)]

    def kernel(slot_ref, *refs):
        ins = refs[:n_mp]
        slope_ref = refs[n_mp]
        downs = refs[n_mp + 1 : n_mp + 1 + nr]
        projs = refs[n_mp + 1 + nr : n_mp + 1 + 2 * nr]
        outs = refs[-len(shapes) :]
        block = jnp.concatenate([ref[...] for ref in ins], axis=0)
        grad_act = grad_heads = 0.0
        for r in range(nr):
            own = block[:, r * part : (r + 1) * part]
            put_rows(outs[r], own)
            grad_act = grad_act + matmul(own, downs[r][...], NN)
            grad_heads = grad_heads + matmul(own, projs[r][...], NN)
        put_rows(outs[nr], grad_act * flat_rows(slope_ref))
        put_rows(outs[nr + 1], grad_heads)

    before = before or []
    operands = list(pieces) + [slope] + list(down) + list(proj)
    return pl.pallas_call(
        kernel,
        out_shape=[jax.ShapeDtypeStruct((n_mp, nz, rows, c), kind) for c, kind in shapes],
        grid_spec=pltpu.PrefetchScalarGridSpec(
            num_scalar_prefetch=1,
            grid=(1,),
            in_specs=[whole_spec(v) for v in pieces]
            + [slot_spec(n_mp, rows, hidden)]
            + [whole_spec(v) for v in list(down) + list(proj)]
            + [pl.BlockSpec(memory_space=pl.ANY)] * len(before),
            out_specs=[slot_spec(n_mp, rows, c) for c, _ in shapes],
        ),
        input_output_aliases={1 + len(operands) + k: k for k in range(len(before))},
        cost_estimate=cost(
            2 * n_mp * rows * width * (hidden + units), 2 * width * (hidden + units + 2 * n_mp * rows)
        ),
        name="back",
    )(slot, *operands, *before)


def attention(qkv, grad_heads, cosine, sine, starts, key_ids, heads):
    n_mp, nz, rows, units = grad_heads.shape
    tokens = n_mp * rows
    size = units // heads
    half_rot = RD // 2

    def kernel(qkv_ref, do_ref, cos_ref, sin_ref, start_ref, key_ref, out_ref, dqkv_ref):
        lane = lax.broadcasted_iota(jnp.int32, (1, units), 1)
        front = lane % size < half_rot
        cos, sin = flat_rows(cos_ref), flat_rows(sin_ref)

        def partner(v):
            return jnp.where(
                front, pltpu.roll(v, units - half_rot, 1), pltpu.roll(v, half_rot, 1)
            )

        rows_qkv = flat_rows(qkv_ref)
        query = rows_qkv[:, :units]
        key = rows_qkv[:, units : 2 * units]
        value = rows_qkv[:, 2 * units :].astype(BF)
        query = (query * cos + partner(query) * sin).astype(BF)
        key = (key * cos + partner(key) * sin).astype(BF)
        scale = jnp.asarray(size ** (-0.5), BF)
        query = query * scale
        grad = flat_rows(do_ref)
        bounds = flat_rows(start_ref)
        ids = key_ref[...]
        allowed = jnp.logical_and(ids <= bounds[:, 0:1], ids >= bounds[:, 1:2])
        attended = dquery = dkey = dvalue = jnp.zeros((tokens, units), F32)
        for h in range(heads):
            here = lane // size == h
            own_q = jnp.where(here, query, 0)
            own_g = jnp.where(here, grad, 0)
            scores = jnp.where(allowed, matmul(own_q, key, NT), neg_large)
            weights = jnp.exp(scores - jnp.max(scores, axis=1, keepdims=True))
            probs = weights * (1.0 / jnp.sum(weights, axis=1, keepdims=True))
            probs_bf = probs.astype(BF)
            attended = jnp.where(here, matmul(probs_bf, value, NN), attended)
            dvalue = dvalue + matmul(probs_bf, own_g, TN)
            dprobs = matmul(own_g, value, NT)
            delta = jnp.sum(probs * dprobs, axis=1, keepdims=True)
            dscores = (probs * (dprobs - delta)).astype(BF)
            dquery = jnp.where(here, matmul(dscores, key, NN), dquery)
            dkey = dkey + matmul(dscores, own_q, TN)
        dquery = dquery * size ** (-0.5)
        put_rows(out_ref, attended)
        dquery = dquery * cos - partner(dquery) * sin
        dkey = dkey * cos - partner(dkey) * sin
        shape = (n_mp, 1, rows, units)
        dqkv_ref[..., :units] = dquery.astype(BF).reshape(shape)
        dqkv_ref[..., units : 2 * units] = dkey.astype(BF).reshape(shape)
        dqkv_ref[..., 2 * units :] = dvalue.astype(BF).reshape(shape)

    spec = functools.partial(rows_spec, n_mp, rows)
    return pl.pallas_call(
        kernel,
        out_shape=[
            jax.ShapeDtypeStruct((n_mp, nz, rows, units), BF),
            jax.ShapeDtypeStruct((n_mp, nz, rows, 3 * units), BF),
        ],
        grid=(nz,),
        in_specs=[
            spec(3 * units),
            spec(units),
            spec(units),
            spec(units),
            spec(2),
            whole_spec(key_ids),
        ],
        out_specs=[spec(units), spec(3 * units)],
        cost_estimate=cost(14 * nz * tokens * tokens * units, 12 * nz * tokens * units * 4),
        name="attention",
    )(qkv, grad_heads, cosine, sine, starts, key_ids)


def back_rows(lefts, weights, first, count, added, kind):
    nr = len(weights[0])
    part = weights[0][0].shape[0]
    block = min(count, 512)
    n_left = len(lefts)
    added = added or []

    def kernel(*refs):
        ins = refs[:n_left]
        blocks = refs[n_left : n_left + n_left * nr]
        extra = refs[n_left + n_left * nr : -nr]
        for r in range(nr):
            total = extra[r][...].astype(F32) if added else 0.0
            for k in range(n_left):
                total = total + matmul(ins[k][...], blocks[k * nr + r][...], NT)
            refs[len(refs) - nr + r][...] = total.astype(kind)

    at = first // block
    width_in = sum(v.shape[1] for v in lefts)
    flat_weights = [v for group in weights for v in group]
    return pl.pallas_call(
        kernel,
        out_shape=[jax.ShapeDtypeStruct((count, part), kind)] * nr,
        grid=(count // block,),
        in_specs=[pl.BlockSpec((block, v.shape[1]), lambda g: (at + g, 0)) for v in lefts]
        + [whole_spec(v) for v in flat_weights]
        + [pl.BlockSpec((block, part), lambda g: (at + g, 0))] * len(added),
        out_specs=[pl.BlockSpec((block, part), lambda g: (g, 0))] * nr,
        cost_estimate=cost(2 * count * width_in * part * nr, 4 * count * part * nr),
        name="back_rows",
    )(*lefts, *flat_weights, *added)


def make_body(sizes):
    nz, nr, nx, nc = (sizes[name] for name in ("z", "r", "x", "c"))

    def fetch(value, axis, step):
        n = sizes[axis]
        step %= n
        if step == 0:
            return value
        return lax.ppermute(value, axis, [((i + step) % n, i) for i in range(n)])

    def body(
        hidden_in,
        lengths,
        norm_gain,
        norm_shift,
        qkv_weight,
        qkv_bias,
        proj_weight,
        proj_bias,
        up_weight,
        up_bias,
        down_weight,
        down_bias,
        cotangent,
    ):
        zi, ri, xi, ci = (lax.axis_index(name) for name in ("z", "r", "x", "c"))
        n_dp, n_mp = nz * nr, nx * nc
        n_all = n_dp * n_mp
        rows, width = hidden_in.shape
        group_rows = rows * n_mp
        head_size = qkv_bias.shape[2] * n_dp
        heads = qkv_bias.shape[1] // nz
        hidden_units = up_weight.shape[1] // nz
        shard = norm_gain.shape[0]

        def to_plane(value):
            lead = value.shape[:-1]
            value = value.reshape(lead + (nz, nr, -1))
            value = jnp.moveaxis(value, -2, len(lead))
            value = jnp.concatenate([value, value], axis=len(lead))
            value = lax.dynamic_slice_in_dim(value, ri, nr, axis=len(lead))
            return value.reshape(lead + (width,))

        def from_plane(value):
            lead = value.shape[:-1]
            value = value.reshape(lead + (nr, nz, -1))
            value = jnp.concatenate([value, value], axis=len(lead))
            value = lax.dynamic_slice_in_dim(value, nr - ri, nr, axis=len(lead))
            return jnp.moveaxis(value, len(lead), -2).reshape(lead + (width,))

        def exchange(value, axes):
            return lax.all_to_all(value, axes, 0, 0, tiled=True)

        ub_rows = up_bias.shape[0] // nz
        small = jnp.concatenate(
            [
                norm_gain,
                norm_shift,
                proj_bias + down_bias,
                up_bias.astype(F32).reshape(-1),
                qkv_bias.astype(F32).reshape(-1),
                lengths.astype(F32).reshape(-1),
            ]
        )
        every = exchange(
            jnp.broadcast_to(small[None], (n_all, small.shape[0])), ("z", "r", "x", "c")
        )
        gain_full = to_plane(every[:, :shard].reshape(width))
        shift_full = to_plane(every[:, shard : 2 * shard].reshape(width))
        bias_full = to_plane(every[:, 2 * shard : 3 * shard].reshape(width))
        mine = lax.dynamic_index_in_dim(
            every.reshape(n_dp, n_mp, -1), xi * nc + ci, axis=1, keepdims=False
        )
        at = 3 * shard
        ub_all = mine[:, at : at + up_bias.size].reshape(n_dp, up_bias.shape[0], up_bias.shape[1])
        ub_all = lax.dynamic_slice_in_dim(ub_all, zi * ub_rows, ub_rows, axis=1)
        ub_all = ub_all.transpose(1, 0, 2).reshape(hidden_units)
        at += up_bias.size
        qb_all = mine[:, at : at + qkv_bias.size].reshape((n_dp,) + qkv_bias.shape)
        qb_all = lax.dynamic_slice_in_dim(qb_all, zi * heads, heads, axis=2)
        qb_all = qb_all.transpose(1, 2, 0, 3).reshape(3 * heads * head_size)
        at += qkv_bias.size
        group_lengths = mine[:, at:].astype(jnp.int32).reshape(nz, nr, -1)
        group_lengths = lax.dynamic_index_in_dim(group_lengths, ri, axis=1, keepdims=False)

        def gather_rows(own):
            groups = []
            for dz in range(nz):
                line = [fetch(own, "x", dx) for dx in range(nx)]
                groups.append([fetch(part, "c", dc) for dc in range(nc) for part in line])
                if dz + 1 < nz:
                    own = fetch(own, "z", 1)
            return groups

        def gather_weight(blocks):
            own = exchange(blocks, "z").reshape(width // nr, blocks.shape[2])
            return [fetch(own, "r", dr) for dr in range(nr)]

        step = width // n_dp
        units = heads * head_size
        tokens = nz * group_rows
        hidden_rows = gather_rows(to_plane(hidden_in))
        qkv_all = gather_weight(
            qkv_weight.reshape(step, 3, nz, units).transpose(2, 0, 1, 3).reshape(nz, step, 3 * units)
        )
        up_all = gather_weight(up_weight.reshape(step, nz, hidden_units).transpose(1, 0, 2))
        grad_rows = gather_rows(to_plane(cotangent))
        both = jnp.concatenate(
            [
                down_weight.T.reshape(step, nz, hidden_units),
                proj_weight.T.reshape(step, nz, units),
            ],
            axis=2,
        ).transpose(1, 0, 2)
        both = gather_weight(both)
        down_all = [v[:, :hidden_units] for v in both]
        proj_all = [v[:, hidden_units:] for v in both]

        normed = None
        for dz in range(nz):
            slot = ((zi + dz) % nz).astype(jnp.int32)[None]
            normed = norm_group(
                slot, hidden_rows[dz], gain_full[None], shift_full[None], normed, nz, nr
            )

        local = jnp.arange(n_mp * rows, dtype=jnp.int32)
        dc, dx, row = local // (nx * rows), (local // rows) % nx, local % rows
        row_ids = (((xi + dx) % nx) * nc + (ci + dc) % nc) * rows + row
        seq_ends = jnp.cumsum(group_lengths, axis=1)
        passed = row_ids[None, :, None] >= seq_ends[:, None, :]
        starts = jnp.max(jnp.where(passed, seq_ends[:, None, :], 0), axis=2)
        by_place = lambda value: value.reshape(nz, n_mp, rows).transpose(1, 0, 2)
        ids = by_place(jnp.broadcast_to(row_ids[None], starts.shape))
        starts = by_place(starts)
        cos, sin = rotary_tables(ids - starts)
        rest = jnp.zeros(cos.shape[:-1] + (head_size - RD,), F32)
        cosine = jnp.concatenate([cos, cos, rest + 1.0] * heads, axis=-1)
        sine = jnp.concatenate([-sin, sin, rest] * heads, axis=-1)
        bounds = jnp.stack([ids, starts], axis=-1)

        (qkv_rows,) = project(normed, qkv_all, qb_all[None], False)
        activated, slope = project(normed, up_all, ub_all[None], True)

        back = None
        for dz in range(nz):
            slot = ((zi + dz) % nz).astype(jnp.int32)[None]
            back = back_group(slot, grad_rows[dz], slope, down_all, proj_all, back)
        grad_plane, grad_pre, grad_heads = back[:nr], back[nr], back[nr + 1]
        attended, grad_qkv = attention(
            qkv_rows, grad_heads, cosine, sine, bounds, row_ids[None], heads
        )
        activated, attended, grad_pre, grad_qkv = (
            v.reshape(tokens, -1) for v in (activated, attended, grad_pre, grad_qkv)
        )

        def scatter_rows(lefts, weights):
            quarter = nz * rows
            sent = back_rows(lefts, weights, nx * quarter, nx * quarter, None, BF)
            got = [fetch(v, "c", -1) for v in sent]
            sent = back_rows(lefts, weights, quarter, quarter, got, BF)
            far = [fetch(v, "x", -1) for v in sent]
            kept = back_rows(lefts, weights, 0, quarter, got, F32)
            parts = []
            for near, other in zip(kept, far):
                line = (near + other.astype(F32)).astype(BF)
                line = exchange(line.reshape(nz, rows, width // nr), "z")
                parts.append(jnp.sum(line.astype(F32), axis=0))
            return jnp.concatenate(parts, axis=1)

        def scatter_weight(lefts, right):
            piece = matmul(lefts[0].reshape(tokens, -1), right, TN)
            for dr in range(1, nr):
                other = matmul(lefts[dr].reshape(tokens, -1), right, TN).astype(BF)
                piece = piece + fetch(other, "r", -dr).astype(F32)
            return exchange(piece.astype(BF).reshape(nz, step, right.shape[1]), "z").astype(F32)

        down_out = scatter_weight(grad_plane, activated).transpose(0, 2, 1)
        down_out = down_out.reshape(nz * hidden_units, step)
        up_out = scatter_weight(normed, grad_pre)
        up_out = up_out.transpose(1, 0, 2).reshape(step, nz * hidden_units)
        grad_local = scatter_rows([grad_pre, grad_qkv], [up_all, qkv_all])
        qkv_out = scatter_weight(normed, grad_qkv)
        qkv_out = qkv_out.reshape(nz, step, 3, units).transpose(1, 2, 0, 3)
        qkv_out = qkv_out.reshape(step, 3, nz * units)
        proj_out = scatter_weight(grad_plane, attended).transpose(0, 2, 1)
        proj_out = proj_out.reshape(nz * units, step)

        branch_sum = scatter_rows([activated, attended], [down_all, proj_all])
        layer_out = from_plane(branch_sum + bias_full)
        inputs32 = hidden_in.astype(F32)
        layer_out = (inputs32 + layer_out).astype(BF)

        col_sums = jnp.concatenate(
            [
                jnp.sum(grad_pre.astype(F32), axis=0).reshape(ub_rows, head_size),
                jnp.sum(grad_qkv.astype(F32), axis=0).reshape(3 * heads, head_size),
            ]
        )
        count = ub_rows + 3 * heads
        block = head_size // n_dp
        col_sums = col_sums.reshape(count, n_dp, block).transpose(1, 0, 2).reshape(n_dp, -1)
        sums = exchange(col_sums, ("z", "r"))
        bias_rows = jnp.sum(sums.reshape(nz, nr, -1), axis=1).reshape(nz, count, block)
        ubias_out = bias_rows[:, :ub_rows].reshape(nz * ub_rows, block)
        qbias_out = bias_rows[:, ub_rows:].reshape(nz, 3, heads, block)
        qbias_out = qbias_out.transpose(1, 0, 2, 3).reshape(3, nz * heads, block)

        standard, inv_scale = standardize(to_plane(hidden_in).astype(F32))
        sums = jnp.stack([jnp.sum(grad_local * standard, axis=0), jnp.sum(grad_local, axis=0)])
        own_sums = jnp.sum(cotangent.astype(F32), axis=0)
        sums = jnp.concatenate([from_plane(sums), own_sums[None]])
        sums = sums.reshape(3, n_all, shard).transpose(1, 0, 2)
        sums = exchange(sums.reshape(n_all, 3 * shard), ("z", "r", "x", "c"))
        gain_out, shift_out, bias_out = jnp.sum(sums, axis=0).reshape(3, shard)
        grad_unit = grad_local * gain_full
        input_grad = inv_scale * (
            grad_unit
            - jnp.mean(grad_unit, axis=1, keepdims=True)
            - standard * jnp.mean(grad_unit * standard, axis=1, keepdims=True)
        )
        input_grad = cotangent.astype(F32) + from_plane(input_grad)
        return (
            layer_out,
            input_grad,
            gain_out,
            shift_out,
            qkv_out,
            qbias_out,
            proj_out,
            bias_out,
            up_out,
            ubias_out,
            down_out,
            bias_out,
        )

    return body


def solution(mesh):
    n_dp, n_mp = mesh.shape["dp"], mesh.shape["mp"]
    sizes = {"z": ZW, "r": n_dp // ZW, "x": XW, "c": n_mp // XW}
    fine = Mesh(mesh.devices.reshape(tuple(sizes.values())), tuple(sizes))
    dp, mp = ("z", "r"), ("x", "c")
    every = dp + mp
    rows, vector = P(every, None), P(every)
    in_specs = (
        rows,
        P(dp, None),
        vector,
        vector,
        P(dp, None, mp),
        P(None, mp, dp),
        P(mp, dp),
        vector,
        P(dp, mp),
        P(mp, dp),
        P(mp, dp),
        vector,
        rows,
    )
    out_specs = (
        rows,
        rows,
        vector,
        vector,
        P(dp, None, mp),
        P(None, mp, dp),
        P(mp, dp),
        vector,
        P(dp, mp),
        P(mp, dp),
        P(mp, dp),
        vector,
    )
    return jax.shard_map(
        make_body(sizes), mesh=fine, in_specs=in_specs, out_specs=out_specs, check_vma=False
    )
```
